32 devices in a mesh: dp: 4 (over z), expert: 4 (over x, core), tensor: 2 (over y).
Axes of the slice: x: 2, y: 2, z: 4, core: 2. Of those that a mesh axis runs over, the one named last changes fastest.
Arguments:
- tokens: bfloat16 [4096, 1536], P(('dp', 'expert')), may hold values from -6 to 6
- lengths: int32 [16], P(('dp', 'expert')), may hold values from 64 to 256, as said below
- expert_ids: int32 [4096, 2], P(('dp', 'expert')), may hold values from 0 to 7, all different within a row; in each aligned block of 256 rows (0 to 255, 256 to 511, ...) at most 80 rows name the same one
- route_gates: float32 [4096, 2], P(('dp', 'expert')), may hold values from 0.5 to 1.5
- cotangent: bfloat16 [4096, 1536], P(('dp', 'expert')), may hold values from -6 to 6
- attn_gain: float32 [1536], replicated, may hold values from 0.25 to 1.75
- w_query: bfloat16 [1536, 1536], P('expert', 'tensor'), may hold values from -0.15625 to 0.15625
- key_projection: bfloat16 [1536, 512], P('expert', 'tensor'), may hold values from -0.15625 to 0.15625
- value_projection: bfloat16 [1536, 512], P('expert', 'tensor'), may hold values from -0.15625 to 0.15625
- w_out: bfloat16 [1536, 1536], P('tensor', 'expert'), may hold values from -1.25 to 1.25
- ffn_gain: float32 [1536], replicated, may hold values from 0.25 to 1.75
- w_gate: bfloat16 [8, 1536, 512], P('expert', None, 'tensor'), may hold values from -0.15625 to 0.15625
- w_up: bfloat16 [8, 1536, 512], P('expert', None, 'tensor'), may hold values from -0.15625 to 0.15625
- w_down: bfloat16 [8, 512, 1536], P('expert', 'tensor'), may hold values from -0.375 to 0.375
Outputs:
- output: bfloat16 [4096, 1536], P(('dp', 'expert'))
- grad_tokens: float32 [4096, 1536], P(('dp', 'expert'))
- grad_attn_gain: float32 [1536], P('expert')
- grad_w_query: float32 [1536, 1536], P('expert', 'tensor')
- grad_w_key: float32 [1536, 512], P('expert', 'tensor')
- grad_w_value: float32 [1536, 512], P('expert', 'tensor')
- grad_w_out: float32 [1536, 1536], P('tensor', 'expert')
- grad_ffn_gain: float32 [1536], P('expert')
- grad_w_gate: float32 [8, 1536, 512], P('expert', None, 'tensor')
- grad_w_up: float32 [8, 1536, 512], P('expert', None, 'tensor')
- grad_w_down: float32 [8, 512, 1536], P('expert', 'tensor')
The draws below stay inside these ranges and needn't reach their ends.
Inputs may be any that keep to these rules, and one draw needn't show every extreme that they name: `lengths`: each used slot count is at least a quarter of 256, and some sequence uses all 256 slots. `expert_ids`: each row names 2 different experts. Among the rows of one sequence no expert is named by more than 80 rows, and in some aligned block of 256 rows some expert is named by exactly 80.
All inputs are finite; a program needn't handle non-finite values.
Results may differ from the reference program's by a relative error of at most 0.014.
Values may be sent and summed in bfloat16 or wider, within the bound.
No kernel may reach another device: no remote copies, remote signals or barrier semaphores. Data moves between devices by JAX's collectives and lax.ppermute only.
A program may use at most 192 MiB of HBM per device.

```python
import math
import jax
import jax.numpy as jnp
import numpy as np
from jax import lax

MODEL_DIMENSION = 1536
QUERY_HEADS = 24
KEY_VALUE_HEADS = 8
HEAD_SIZE = 64
FF = 512
TOKEN_SLOTS = 256
EXPERTS = 8
TOP = 2
CAP = 80
SEQS = 16
TOKENS = 4096


def draw_lengths(key, part):
    values = jax.random.randint(key, (SEQS,), TOKEN_SLOTS // 4, TOKEN_SLOTS + 1)
    longest = jax.random.randint(jax.random.fold_in(key, 7), (), 0, SEQS)
    return values.at[longest].set(TOKEN_SLOTS).astype(jnp.int32)


def shard_levels(own_key, shape, pieces, low, top_value):
    gain, own = 1.0, jax.random.fold_in(own_key, 6)
    for dim, parts in pieces:
        steps = jnp.exp(jax.random.uniform(jax.random.fold_in(own, dim), (parts,), jnp.float32, low / len(pieces), top_value / len(pieces)))
        gain = gain * jnp.repeat(steps, shape[dim] // parts).reshape([-1 if axis == dim else 1 for axis in range(len(shape))])
    return gain


def routed_block(stream_key, own, number, rows, number_of, top, limit, skew):
    sequence = jax.random.permutation(stream_key, number_of)
    crowded, common = portions_of(number_of, rows * top, limit, skew, True), portions_of(number_of, rows * top, limit, skew, False)
    places = jnp.arange(number_of)

    def named(tallies, offset_by):
        used = int((tallies > 0).sum())
        fixed = max(1, used // 4)
        moved = fixed + (places - fixed + offset_by * (used - fixed)) % max(1, number_of - fixed)
        return jnp.zeros((number_of,), jnp.int32).at[sequence[jnp.where(places < fixed, places, moved)]].set(jnp.asarray(tallies, jnp.int32))

    tallies = jnp.where(number % 4 == 0, named(crowded, number // 4), named(common, number - number // 4 - 1))
    mixed = jax.random.permutation(jax.random.fold_in(own, 3), number_of)
    giver, sink = mixed[0:number_of // 2 * 2:2], mixed[1:number_of // 2 * 2:2]
    margin = jnp.minimum(tallies[giver] - 1, limit - tallies[sink]) // 2
    margin = jnp.where((giver == sequence[0]) | (sink == sequence[0]) | (tallies[sink] == 0), 0, jnp.maximum(margin, 0))
    moved = jax.random.randint(jax.random.fold_in(own, 4), (number_of // 2,), 0, 1 << 20) % (margin + 1)
    tallies = tallies.at[giver].add(-moved).at[sink].add(moved)
    items = jnp.searchsorted(jnp.cumsum(tallies), jnp.arange(rows * top), side="right").astype(jnp.int32)
    table = items.reshape(top, rows).T
    table = table[jax.random.permutation(jax.random.fold_in(own, 1), rows)]
    offset_by = jax.random.randint(jax.random.fold_in(own, 2), (rows, 1), 0, top)
    return jnp.take_along_axis(table, (jnp.arange(top)[None, :] + offset_by) % top, axis=1)


def portions_of(count, total, most, lean, full):
    loads = [(1 << 20) // math.isqrt(grade ** lean) + 1 for grade in range(1, count + 1)]
    largest = most if full else min(most, max(-(-total // count), total * loads[0] // sum(loads)))
    least = 1 if total - largest >= count - 1 else 0
    counts, rest = [largest] + [least] * (count - 1), total - largest - least * (count - 1)
    while rest > 0:
        movable = [i for i in range(1, count) if counts[i] < largest] or [i for i in range(1, count) if counts[i] < most]
        mass, remaining = sum([loads[i] for i in movable]), rest
        for i in movable:
            addition = min(most - counts[i], max(1, remaining * loads[i] // mass), rest)
            counts[i] = counts[i] + addition
            rest = rest - addition
    return np.array(counts)


def noise(stream_key, dims, deviation, most, shards=(), kind=jnp.bfloat16):
    array = deviation * jax.random.normal(stream_key, dims, jnp.float32)
    if shards:
        array = array * shard_levels(stream_key, dims, shards, -0.22, 0.18)
    return jnp.clip(array, -most, most).astype(kind)


def setup_inputs(seed: int = 0) -> dict:
    key_of = jax.random.split(jax.random.key(seed), 15)
    tokens = noise(key_of[0], (TOKENS, MODEL_DIMENSION), 1.0, 6.0, ((0, 16),))
    lengths = draw_lengths(jax.random.fold_in(key_of[14], 71), 0)
    expert_ids_keys = jax.random.split(jax.random.fold_in(key_of[2], 1), TOKENS // TOKEN_SLOTS)
    expert_ids_turns = jax.random.permutation(jax.random.fold_in(key_of[2], 3), TOKENS // TOKEN_SLOTS)
    expert_ids = jax.vmap(lambda own, number: routed_block(jax.random.fold_in(key_of[2], 2), own, number, TOKEN_SLOTS, EXPERTS, TOP, CAP, 1))(expert_ids_keys, expert_ids_turns).reshape((TOKENS, TOP))
    route_gates = jnp.clip(0.5 + 1.0 * jax.random.uniform(key_of[3], (TOKENS, TOP), jnp.float32) ** shard_levels(key_of[3], (TOKENS, TOP), ((0, 16),), -0.2, 0.2), 0.5, 1.5)
    cotangent = noise(key_of[4], (TOKENS, MODEL_DIMENSION), 1.0, 6.0, ((0, 16),))
    attn_gain = jnp.clip(1.0 + 0.15 * jax.random.normal(key_of[5], (MODEL_DIMENSION,), jnp.float32), 0.25, 1.75)
    w_query = noise(key_of[6], (MODEL_DIMENSION, QUERY_HEADS * HEAD_SIZE), MODEL_DIMENSION ** -0.5, 0.15625, ((0, 4), (1, 2)))
    key_projection = noise(key_of[7], (MODEL_DIMENSION, KEY_VALUE_HEADS * HEAD_SIZE), MODEL_DIMENSION ** -0.5, 0.15625, ((0, 4), (1, 2)))
    value_projection = noise(key_of[8], (MODEL_DIMENSION, KEY_VALUE_HEADS * HEAD_SIZE), MODEL_DIMENSION ** -0.5, 0.15625, ((0, 4), (1, 2)))
    w_out = noise(key_of[9], (QUERY_HEADS * HEAD_SIZE, MODEL_DIMENSION), (QUERY_HEADS * HEAD_SIZE // 64) ** -0.5, 1.25, ((0, 2), (1, 4)))
    ffn_gain = jnp.clip(1.0 + 0.15 * jax.random.normal(key_of[10], (MODEL_DIMENSION,), jnp.float32), 0.25, 1.75)
    w_gate = noise(key_of[11], (EXPERTS, MODEL_DIMENSION, FF), MODEL_DIMENSION ** -0.5, 0.15625, ((0, 4), (2, 2)))
    w_up = noise(key_of[12], (EXPERTS, MODEL_DIMENSION, FF), MODEL_DIMENSION ** -0.5, 0.15625, ((0, 4), (2, 2)))
    w_down = noise(key_of[13], (EXPERTS, FF, MODEL_DIMENSION), (FF // 2) ** -0.5, 0.375, ((0, 4), (1, 2)))
    return {"tokens": tokens, "lengths": lengths, "expert_ids": expert_ids, "route_gates": route_gates, "cotangent": cotangent, "attn_gain": attn_gain, "w_query": w_query, "key_projection": key_projection, "value_projection": value_projection, "w_out": w_out, "ffn_gain": ffn_gain, "w_gate": w_gate, "w_up": w_up, "w_down": w_down}


norm_eps = 1e-06
rope_base = 10000.0
masked_score = -1e+30

@jax.custom_vjp
def reduced_input(v):
    return lax.optimization_barrier(v.astype(jnp.bfloat16)).astype(jnp.float32)

@jax.custom_vjp
def reduced_gradient(v):
    return v

def low_keep(v):
    return (reduced_input(v), None)

def low_pass(kept, grad):
    return (grad,)

def back_keep(v):
    return (v, None)

def back_low(kept, grad):
    return (reduced_input(grad),)
reduced_input.defvjp(low_keep, low_pass)
reduced_gradient.defvjp(back_keep, back_low)

def rms_scale(values, gain_vec):
    inverse = lax.rsqrt(lax.optimization_barrier(jnp.mean(values * values, axis=-1, keepdims=True)) + norm_eps)
    return values * inverse * gain_vec

def rope_tables(seq_len, head_dim):
    half_dim = head_dim // 2
    frequencies = rope_base ** (-(jnp.arange(half_dim, dtype=jnp.float32) * 2.0 / head_dim))
    angles = jnp.arange(seq_len, dtype=jnp.float32)[:, None] * frequencies[None, :]
    return (jnp.cos(angles)[:, None, :], jnp.sin(angles)[:, None, :])

def rotate(values, cosine_table, sine_table):
    half_dim = values.shape[-1] // 2
    front_half = values[..., :half_dim]
    back_half = values[..., half_dim:]
    return jnp.concatenate([front_half * cosine_table - back_half * sine_table, back_half * cosine_table + front_half * sine_table], axis=-1)

def precise_product(left, right):
    return jnp.dot(left, right, precision=lax.Precision.HIGHEST)

def reference(tokens, lengths, expert_ids, route_gates, cotangent, attn_gain, w_query, key_projection, value_projection, w_out, ffn_gain, w_gate, w_up, w_down):
    positions = jnp.arange(TOKEN_SLOTS, dtype=jnp.int32)
    used = (positions[None, :] < lengths[:, None]).astype(jnp.float32).reshape(SEQS * TOKEN_SLOTS)
    cosine_table, sine_table = rope_tables(TOKEN_SLOTS, HEAD_SIZE)
    score_scale = HEAD_SIZE ** (-0.5)
    group_width = QUERY_HEADS // KEY_VALUE_HEADS
    combine_all = route_gates * used[:, None]

    def forward(inputs, gain_one, query_w, key_matrix, value_matrix, out_w, gain_two, gate_w, up_w, down_w):
        normed = reduced_input(rms_scale(inputs, gain_one))

        def attend(entry):
            sequence_rows, length = entry
            queries = reduced_gradient(precise_product(sequence_rows, query_w)).reshape(TOKEN_SLOTS, QUERY_HEADS, HEAD_SIZE)
            queries = reduced_input(rotate(queries, cosine_table, sine_table) * score_scale)
            rotated_keys = reduced_gradient(precise_product(sequence_rows, key_matrix)).reshape(TOKEN_SLOTS, KEY_VALUE_HEADS, HEAD_SIZE)
            rotated_keys = reduced_input(rotate(rotated_keys, cosine_table, sine_table))
            reduced_values = reduced_input(reduced_gradient(precise_product(sequence_rows, value_matrix))).reshape(TOKEN_SLOTS, KEY_VALUE_HEADS, HEAD_SIZE)
            rotated_keys = jnp.repeat(rotated_keys, group_width, axis=1)
            reduced_values = jnp.repeat(reduced_values, group_width, axis=1)
            scores = reduced_gradient(jnp.einsum('qhd,khd->hqk', queries, rotated_keys, precision=lax.Precision.HIGHEST))
            allowed = (positions[None, :] <= positions[:, None]) & (positions[None, :] < length)
            scores = jnp.where(allowed[None], scores, masked_score)
            row_peak = lax.optimization_barrier(jnp.max(scores, axis=-1, keepdims=True))
            exp_scores = jnp.exp(scores - row_peak)
            probs_low = reduced_input(exp_scores / lax.optimization_barrier(jnp.sum(exp_scores, axis=-1, keepdims=True)))
            mixed_heads = jnp.einsum('hqk,khd->qhd', probs_low, reduced_values, precision=lax.Precision.HIGHEST)
            return reduced_input(reduced_gradient(mixed_heads)).reshape(TOKEN_SLOTS, QUERY_HEADS * HEAD_SIZE)
        mixed = lax.map(jax.checkpoint(attend), (normed.reshape(SEQS, TOKEN_SLOTS, MODEL_DIMENSION), lengths))
        mixed = mixed.reshape(SEQS * TOKEN_SLOTS, QUERY_HEADS * HEAD_SIZE)
        residual = inputs + reduced_gradient(precise_product(mixed, out_w))
        ffn_in = reduced_input(rms_scale(residual, gain_two))

        def one_expert(running, entry):
            expert_index, gate_one, up_one, down_one = entry
            combine = lax.optimization_barrier(jnp.sum(combine_all * (expert_ids == expert_index).astype(jnp.float32), axis=1))
            expert_rows = reduced_gradient(ffn_in)
            gate_pre = reduced_gradient(precise_product(expert_rows, gate_one))
            up_pre = reduced_gradient(precise_product(expert_rows, up_one))
            hidden = reduced_input(jax.nn.silu(gate_pre) * up_pre)
            part_rows = reduced_input(reduced_gradient(precise_product(hidden, down_one)))
            return (running + combine[:, None] * part_rows, None)
        expert_sum, _ = lax.scan(jax.checkpoint(one_expert), jnp.zeros_like(residual), (jnp.arange(EXPERTS, dtype=jnp.int32), gate_w, up_w, down_w))
        return residual + expert_sum
    params = (tokens.astype(jnp.float32), attn_gain.astype(jnp.float32), w_query.astype(jnp.float32), key_projection.astype(jnp.float32), value_projection.astype(jnp.float32), w_out.astype(jnp.float32), ffn_gain.astype(jnp.float32), w_gate.astype(jnp.float32), w_up.astype(jnp.float32), w_down.astype(jnp.float32))
    result, pullback = jax.vjp(forward, *params)
    grads = pullback(cotangent.astype(jnp.float32))
    return (result.astype(jnp.bfloat16), grads[0], grads[1], grads[2], grads[3], grads[4], grads[5], grads[6], grads[7], grads[8], grads[9])
```

```python
import functools

import jax
import jax.numpy as jnp
import numpy as np
from jax import lax
from jax.experimental import pallas as pl
from jax.experimental.pallas import tpu as pltpu
from jax.sharding import PartitionSpec as P

HEAD_SIZE = 64
norm_eps = 1e-06
rope_base = 10000.0
masked_score = -1e30
LOW = jnp.bfloat16
WIDE = jnp.float32
VMEM = pl.BlockSpec(memory_space=pltpu.VMEM)
SMEM = pl.BlockSpec(memory_space=pltpu.SMEM)


def dot(a, b):
    return lax.dot_general(a, b, (((1,), (0,)), ((), ())), preferred_element_type=WIDE)


def dot_t(a, b):
    return lax.dot_general(a, b, (((1,), (1,)), ((), ())), preferred_element_type=WIDE)


def dot_l(a, b):
    return lax.dot_general(a, b, (((0,), (0,)), ((), ())), preferred_element_type=WIDE)


def xor_pairs(n, bit):
    return [(i, i ^ bit) for i in range(n)]


def swap(values, axis, bit=1):
    return lax.ppermute(values, axis, xor_pairs(lax.axis_size(axis), bit))


def gather_blocks(values, axis="expert"):
    n = lax.axis_size(axis)
    blocks = {0: values}
    bit = n // 2
    while bit:
        for k in list(blocks):
            blocks[k ^ bit] = swap(blocks[k], axis, bit)
        bit //= 2
    return [blocks[k] for k in range(n)]


def add_low(a, b):
    return (a.astype(WIDE) + b.astype(WIDE)).astype(a.dtype)


def scatter_blocks(blocks, axis="expert"):
    n = lax.axis_size(axis)
    blocks = list(blocks)
    bit = 1
    while bit < n:
        for k in reversed(range(0, n, bit)):
            if k & bit:
                blocks[k ^ bit] = add_low(blocks[k ^ bit], swap(blocks[k], axis, bit))
        bit *= 2
    return blocks[0]


def fold_sum(piece, axis="dp"):
    n = lax.axis_size(axis)
    me = lax.axis_index(axis)
    half = n // 2
    total = piece
    for j in range(half - 1):
        total = add_low(total, lax.ppermute(total, axis, [(j, j + 1), (n - 1 - j, n - 2 - j)]))
    total = add_low(total, lax.ppermute(total, axis, [(half - 1, half), (half, half - 1)]))
    for j in range(half - 1):
        came = lax.ppermute(
            total, axis, [(half - 1 - j, half - 2 - j), (half + j, half + j + 1)]
        )
        total = jnp.where((me == half - 2 - j) | (me == half + j + 1), came, total)
    return total


def after(values, *earlier):
    return lax.optimization_barrier((values, earlier))[0]


def rope_tables(seq_len):
    half = HEAD_SIZE // 2
    frequencies = np.float32(rope_base) ** (
        -(np.arange(half, dtype=np.float32) * np.float32(2.0) / np.float32(HEAD_SIZE))
    )
    angles = np.arange(seq_len, dtype=np.float32)[:, None] * frequencies[None, :].astype(np.float32)
    angles = np.tile(angles.astype(np.float64), (1, 128 // half))
    return np.cos(angles).astype(np.float32), np.sin(angles).astype(np.float32)


def turn(values):
    lane = lax.broadcasted_iota(jnp.int32, values.shape, 1) % HEAD_SIZE
    return jnp.where(
        lane < HEAD_SIZE // 2,
        -pltpu.roll(values, 128 - HEAD_SIZE // 2, axis=1),
        pltpu.roll(values, HEAD_SIZE // 2, axis=1),
    )


def part(order, k, count, width):
    if count == 1:
        return pl.ds(0, width)
    return pl.ds(pl.multiple_of(order[k] * width, 128), width)


def allowed_mask(seq_len, length):
    row = lax.broadcasted_iota(jnp.int32, (seq_len, seq_len), 0)
    col = lax.broadcasted_iota(jnp.int32, (seq_len, seq_len), 1)
    return (col <= row) & (col < length)


def stack_heads(ref, group, width):
    return jnp.concatenate(
        [
            ref[:, (group * width + i) * HEAD_SIZE : (group * width + i + 1) * HEAD_SIZE]
            for i in range(width)
        ],
        axis=0,
    )


def probabilities(queries, keys, allowed, width):
    seq_len = keys.shape[0]
    scores = dot_t(queries, keys).reshape(width, seq_len, seq_len)
    scores = jnp.where(allowed[None], scores, masked_score)
    exps = jnp.exp(scores - jnp.max(scores, axis=-1, keepdims=True))
    probs = exps / jnp.sum(exps, axis=-1, keepdims=True)
    return probs.reshape(width * seq_len, seq_len)


def attn_forward_kernel(count, groups, width, order, length, tok, gain, cos, sin, *refs):
    weights, (normed, qkv, mixed, wide) = refs[:count], refs[count:]
    seq_len = tok.shape[0]
    values = tok[...].astype(WIDE)
    inverse = lax.rsqrt(jnp.mean(values * values, axis=-1, keepdims=True) + norm_eps)
    normed[...] = (values * inverse * gain[...]).astype(LOW)
    rows = weights[0].shape[0]
    for k in range(count):
        term = dot(normed[:, part(order, k, count, rows)], weights[k][...])
        if k == 0:
            wide[...] = term
        else:
            wide[...] += term
    q_cols = groups * width * HEAD_SIZE
    k_cols = groups * HEAD_SIZE
    for c in range(0, q_cols + 2 * k_cols, 128):
        piece = wide[:, c : c + 128]
        if c < q_cols + k_cols:
            piece = piece * cos[...] + turn(piece) * sin[...]
        if c < q_cols:
            piece = piece * (HEAD_SIZE**-0.5)
        qkv[:, c : c + 128] = piece.astype(LOW)
    allowed = allowed_mask(seq_len, length[0])
    for g in range(groups):
        queries = stack_heads(qkv, g, width)
        keys = qkv[:, q_cols + g * HEAD_SIZE : q_cols + (g + 1) * HEAD_SIZE]
        at = q_cols + k_cols + g * HEAD_SIZE
        probs = probabilities(queries, keys, allowed, width)
        heads = dot(probs.astype(LOW), qkv[:, at : at + HEAD_SIZE]).astype(LOW)
        for i in range(width):
            h = g * width + i
            mixed[:, h * HEAD_SIZE : (h + 1) * HEAD_SIZE] = heads[i * seq_len : (i + 1) * seq_len]


def attn_forward(order, length, tokens, gain, cos, sin, weights, groups, width):
    seq_len, model_width = tokens.shape
    columns = weights[0].shape[1]
    count = len(weights)
    return pl.pallas_call(
        functools.partial(attn_forward_kernel, count, groups, width),
        out_shape=(
            jax.ShapeDtypeStruct((seq_len, model_width), LOW),
            jax.ShapeDtypeStruct((seq_len, columns), LOW),
            jax.ShapeDtypeStruct((seq_len, groups * width * HEAD_SIZE), LOW),
        ),
        in_specs=[SMEM, SMEM] + [VMEM] * (4 + count),
        out_specs=(VMEM,) * 3,
        scratch_shapes=[pltpu.VMEM((seq_len, columns), WIDE)],
        name="attn_forward",
    )(order, length, tokens, gain, cos, sin, *weights)


def attn_out_kernel(count, order, mixed, *refs):
    weights, (out,) = refs[:count], refs[count:]
    cols = weights[0].shape[1]
    for k in range(count):
        out[:, part(order, k, count, cols)] = dot(mixed[...], weights[k][...]).astype(LOW)


def attn_out(order, mixed, weights):
    count = len(weights)
    model_width = count * weights[0].shape[1]
    return pl.pallas_call(
        functools.partial(attn_out_kernel, count),
        out_shape=jax.ShapeDtypeStruct((mixed.shape[0], model_width), LOW),
        in_specs=[SMEM] + [VMEM] * (1 + count),
        out_specs=VMEM,
        name="attn_out",
    )(order, mixed, *weights)


def residual_kernel(tok, own, other, gain, residual, normed):
    values = tok[...].astype(WIDE) + (own[...].astype(WIDE) + other[...].astype(WIDE))
    residual[...] = values
    inverse = lax.rsqrt(jnp.mean(values * values, axis=-1, keepdims=True) + norm_eps)
    normed[...] = (values * inverse * gain[...]).astype(LOW)


def row_grid(kernel, shapes, rows, args, fixed, accumulated=0, name=None):
    seq_len = args[0].shape[0]
    cut = lambda shape: pl.BlockSpec((rows, shape[1]), lambda i: (i, 0))
    whole = lambda shape: pl.BlockSpec(shape, lambda i: (0, 0))
    outs = [
        cut(s.shape) if i < len(shapes) - accumulated else whole(s.shape)
        for i, s in enumerate(shapes)
    ]
    return pl.pallas_call(
        kernel,
        grid=(seq_len // rows,),
        out_shape=tuple(shapes),
        in_specs=[cut(a.shape) for a in args] + [whole(f.shape) for f in fixed],
        out_specs=tuple(outs),
        name=name,
    )(*args, *fixed)


def expert_kernel(blocks, first, last, *refs):
    h_refs, refs = refs[:blocks], refs[blocks:]
    d_refs, refs = refs[:blocks], refs[blocks:]
    (c_ref, wg, wu, wd), refs = refs[:4], refs[4:]
    if not first:
        before, refs = refs[:3], refs[3:]
    m_outs, refs = refs[:blocks], refs[blocks:]
    r_outs, refs = refs[:blocks], refs[blocks:]
    grads, (m_sum, r_sum) = refs[:3], refs[3:]
    j = pl.program_id(0)
    sums = [None] * 3
    for b in range(blocks):
        rows, outs = h_refs[b][...], d_refs[b][...]
        lane = lax.broadcasted_iota(jnp.int32, c_ref.shape[1:], 1)
        c = jnp.sum(jnp.where(lane == j, c_ref[b], 0.0), axis=1, keepdims=True)
        gate, up = dot(rows, wg[0]), dot(rows, wu[0])
        sig = 1.0 / (1.0 + jnp.exp(-gate))
        silu = gate * sig
        hidden = (silu * up * c).astype(LOW)
        back = dot_t(outs, wd[0]) * c
        grad_gate = (back * up * (sig * (1.0 + gate * (1.0 - sig)))).astype(LOW)
        grad_up = (back * silu).astype(LOW)
        m_term = dot(hidden, wd[0])
        r_term = dot_t(grad_gate, wg[0]) + dot_t(grad_up, wu[0])

        @pl.when(j == 0)
        def _(b=b, m_term=m_term, r_term=r_term):
            m_sum[b] = m_term
            r_sum[b] = r_term

        @pl.when(j > 0)
        def _(b=b, m_term=m_term, r_term=r_term):
            m_sum[b] += m_term
            r_sum[b] += r_term

        for i, term in enumerate(
            (dot_l(rows, grad_gate), dot_l(rows, grad_up), dot_l(hidden, outs))
        ):
            sums[i] = term if sums[i] is None else sums[i] + term
    for i in range(3):
        total = sums[i] if first else sums[i] + before[i][0]
        grads[i][0] = total.astype(grads[i].dtype)

    @pl.when(j == pl.num_programs(0) - 1)
    def _():
        for b in range(blocks):
            m_outs[b][...] = m_sum[b].astype(LOW)
            r_outs[b][...] = r_sum[b].astype(LOW)


def experts(rows, outs, c, w_gate, w_up, w_down, before, last):
    blocks = len(rows)
    seq_len, model_width = rows[0].shape
    local = w_gate.shape[0]
    whole = pl.BlockSpec((seq_len, model_width), lambda j: (0, 0))
    of = lambda w: pl.BlockSpec((1,) + w.shape[1:], lambda j: (j, 0, 0))
    kind = LOW if last else WIDE
    weights = (w_gate, w_up, w_down)
    result = pl.pallas_call(
        functools.partial(expert_kernel, blocks, before is None, last),
        grid=(local,),
        out_shape=tuple(
            [jax.ShapeDtypeStruct((seq_len, model_width), LOW)] * (2 * blocks)
            + [jax.ShapeDtypeStruct(w.shape, kind) for w in weights]
        ),
        in_specs=[whole] * (2 * blocks)
        + [pl.BlockSpec(c.shape, lambda j: (0, 0, 0))]
        + [of(w) for w in weights]
        + ([] if before is None else [of(w) for w in weights]),
        out_specs=tuple([whole] * (2 * blocks) + [of(w) for w in weights]),
        scratch_shapes=[pltpu.VMEM((blocks, seq_len, model_width), WIDE)] * 2,
        name="experts",
    )(*rows, *outs, c, *weights, *(() if before is None else before))
    return result[:blocks], result[blocks : 2 * blocks], result[2 * blocks :]


def norm_back(values, gain, grads):
    inverse = lax.rsqrt(jnp.mean(values * values, axis=-1, keepdims=True) + norm_eps)
    unit = values * inverse
    scaled = grads * gain
    back = inverse * (scaled - unit * jnp.mean(scaled * unit, axis=-1, keepdims=True))
    return back, jnp.sum(grads * unit, axis=0, keepdims=True)


def attn_backward_kernel(
    count, groups, width, order, length, own, other, residual, cot, gain, cos, sin, qkv, *refs
):
    weights, (low, wide, gain_grad, out, do_ref, dq_ref) = refs[:count], refs[count:]
    seq_len = residual.shape[0]
    for r in range(0, seq_len, 64):
        at = pl.ds(r, 64)
        back, part_gain = norm_back(
            residual[at, :], gain[...], own[at, :].astype(WIDE) + other[at, :].astype(WIDE)
        )
        back = back + cot[at, :].astype(WIDE)
        wide[at, :] = back
        low[at, :] = back.astype(LOW)
        if r == 0:
            gain_grad[...] = part_gain
        else:
            gain_grad[...] += part_gain
    cols = weights[0].shape[1]
    total = None
    for k in range(count):
        term = dot_t(low[:, part(order, k, count, cols)], weights[k][...])
        total = term if total is None else total + term
    do_ref[...] = total.astype(LOW)
    q_cols = groups * width * HEAD_SIZE
    k_cols = groups * HEAD_SIZE
    allowed = allowed_mask(seq_len, length[0])
    for g in range(groups):
        k_at, v_at = q_cols + g * HEAD_SIZE, q_cols + k_cols + g * HEAD_SIZE
        queries = stack_heads(qkv, g, width)
        keys, vals = qkv[:, k_at : k_at + HEAD_SIZE], qkv[:, v_at : v_at + HEAD_SIZE]
        grads = stack_heads(do_ref, g, width)
        probs = probabilities(queries, keys, allowed, width)
        grad_probs = dot_t(grads, vals)
        center = jnp.sum(probs * grad_probs, axis=-1, keepdims=True)
        grad_scores = (probs * (grad_probs - center)).astype(LOW)
        grad_queries = dot(grad_scores, keys)
        for i in range(width):
            h = g * width + i
            dq_ref[:, h * HEAD_SIZE : (h + 1) * HEAD_SIZE] = grad_queries[
                i * seq_len : (i + 1) * seq_len
            ]
        dq_ref[:, k_at : k_at + HEAD_SIZE] = dot_l(grad_scores, queries)
        dq_ref[:, v_at : v_at + HEAD_SIZE] = dot_l(probs.astype(LOW), grads)
    for c in range(0, q_cols + 2 * k_cols, 128):
        piece = dq_ref[:, c : c + 128]
        if c < q_cols + k_cols:
            piece = piece * cos[...] - turn(piece) * sin[...]
        if c < q_cols:
            piece = piece * (HEAD_SIZE**-0.5)
        out[:, c : c + 128] = piece.astype(LOW)


def attn_backward(
    order, length, own, other, residual, cot, gain, cos, sin, qkv, weights, groups, width
):
    seq_len, model_width = residual.shape
    count = len(weights)
    q_cols = groups * width * HEAD_SIZE
    return pl.pallas_call(
        functools.partial(attn_backward_kernel, count, groups, width),
        out_shape=(
            jax.ShapeDtypeStruct((seq_len, model_width), LOW),
            jax.ShapeDtypeStruct((seq_len, model_width), WIDE),
            jax.ShapeDtypeStruct((1, model_width), WIDE),
            jax.ShapeDtypeStruct(qkv.shape, LOW),
        ),
        in_specs=[SMEM, SMEM] + [VMEM] * (8 + count),
        out_specs=(VMEM,) * 4,
        scratch_shapes=[pltpu.VMEM((seq_len, q_cols), LOW), pltpu.VMEM(qkv.shape, WIDE)],
        name="attn_backward",
    )(order, length, own, other, residual, cot, gain, cos, sin, qkv, *weights)


def normed_back_kernel(count, order, grads, *refs):
    weights, (out,) = refs[:count], refs[count:]
    rows = weights[0].shape[0]
    for k in range(count):
        out[:, part(order, k, count, rows)] = dot_t(grads[...], weights[k][...]).astype(LOW)


def normed_back(order, grads, weights):
    count = len(weights)
    return pl.pallas_call(
        functools.partial(normed_back_kernel, count),
        out_shape=jax.ShapeDtypeStruct((grads.shape[0], count * weights[0].shape[0]), LOW),
        in_specs=[SMEM] + [VMEM] * (1 + count),
        out_specs=VMEM,
        name="normed_back",
    )(order, grads, *weights)


def input_kernel(own, other, tok, upstream, gain, out, gain_grad):
    back, part_gain = norm_back(
        tok[...].astype(WIDE), gain[...], own[...].astype(WIDE) + other[...].astype(WIDE)
    )
    out[...] = upstream[...] + back
    i = pl.program_id(0)

    @pl.when(i == 0)
    def _():
        gain_grad[...] = part_gain

    @pl.when(i > 0)
    def _():
        gain_grad[...] += part_gain


def pair_dot_kernel(count, *refs):
    left, right, (out,) = refs[:count], refs[count : 2 * count], refs[2 * count :]
    total = None
    for k in range(count):
        term = dot_l(left[k][...], right[k][...])
        total = term if total is None else total + term
    out[...] = total.astype(LOW)


def pair_dot(left, right, name):
    count = len(left)
    return pl.pallas_call(
        functools.partial(pair_dot_kernel, count),
        out_shape=jax.ShapeDtypeStruct((left[0].shape[1], right[0].shape[1]), LOW),
        in_specs=[VMEM] * (2 * count),
        out_specs=VMEM,
        name=name,
    )(*left, *right)


def body(
    tokens,
    lengths,
    expert_ids,
    route_gates,
    cotangent,
    attn_gain,
    w_query,
    key_projection,
    value_projection,
    w_out,
    ffn_gain,
    w_gate,
    w_up,
    w_down,
):
    seq_len, model_width = tokens.shape
    owners = lax.axis_size("expert")
    mine = lax.axis_index("expert")
    local_experts = w_gate.shape[0]
    experts_all = local_experts * owners
    groups = key_projection.shape[1] // HEAD_SIZE
    width = w_query.shape[1] // key_projection.shape[1]
    shard = w_query.shape[0]
    aligned = shard % 128 == 0 and owners & (owners - 1) == 0
    cos, sin = rope_tables(seq_len)
    gain_one, gain_two = attn_gain[None, :], ffn_gain[None, :]

    proj = jnp.concatenate([w_query, key_projection, value_projection], axis=1)
    if aligned:
        order = jnp.arange(owners, dtype=jnp.int32) ^ mine
        proj_blocks = gather_blocks(proj)
        out_blocks = gather_blocks(after(w_out, proj_blocks[owners // 2]))
    else:
        order = jnp.zeros((1,), jnp.int32)
        proj_blocks = [lax.all_gather(proj, "expert", axis=0, tiled=True)]
        out_blocks = [lax.all_gather(w_out, "expert", axis=1, tiled=True)]

    used = jnp.arange(seq_len, dtype=jnp.int32) < lengths[0]
    named = expert_ids[:, :, None] == jnp.arange(experts_all, dtype=jnp.int32)[None, None, :]
    combine = jnp.sum(jnp.where(named, route_gates[:, :, None], 0.0), axis=1)
    combine = jnp.where(used[:, None], combine, 0.0).T
    combine = jnp.stack(gather_blocks(combine))
    combine = lax.dynamic_slice_in_dim(combine, mine * local_experts, local_experts, 1)
    combine = jnp.swapaxes(combine, 1, 2)
    cot_blocks = gather_blocks(after(cotangent, out_blocks[-1]))

    normed, qkv, mixed = attn_forward(
        order, lengths, tokens, gain_one, cos, sin, proj_blocks, groups, width
    )
    attn_own = attn_out(order, mixed, out_blocks)
    attn_other = swap(attn_own, "tensor")
    residual, ffn_low = row_grid(
        residual_kernel,
        [
            jax.ShapeDtypeStruct((seq_len, model_width), WIDE),
            jax.ShapeDtypeStruct((seq_len, model_width), LOW),
        ],
        64,
        [tokens, attn_own, attn_other],
        [gain_two],
        name="residual",
    )

    ffn_blocks = gather_blocks(ffn_low)
    m_blocks, r_blocks, grads = [None] * owners, [None] * owners, None
    step = min(2, owners)
    for k in range(0, owners, step):
        m_part, r_part, grads = experts(
            ffn_blocks[k : k + step],
            cot_blocks[k : k + step],
            combine[k : k + step],
            w_gate,
            w_up,
            w_down,
            grads,
            k + step == owners,
        )
        m_blocks[k : k + step], r_blocks[k : k + step] = m_part, r_part

    flat = lambda a: a.reshape(-1, a.shape[-1])
    sums = []
    for g in grads:
        sums.append([fold_sum(g[j]) for j in range(local_experts)])

    r_own = scatter_blocks(r_blocks)
    r_other = swap(r_own, "tensor")
    low, upstream, ffn_gain_part, grad_qkv = attn_backward(
        order,
        lengths,
        r_own,
        r_other,
        residual,
        cotangent,
        gain_two,
        cos,
        sin,
        qkv,
        out_blocks,
        groups,
        width,
    )
    grad_own = normed_back(order, grad_qkv, proj_blocks)
    grad_other = swap(grad_own, "tensor")
    grad_tokens, attn_gain_part = row_grid(
        input_kernel,
        [
            jax.ShapeDtypeStruct((seq_len, model_width), WIDE),
            jax.ShapeDtypeStruct((1, model_width), WIDE),
        ],
        64,
        [grad_own, grad_other, tokens, upstream],
        [gain_one],
        accumulated=1,
        name="input_grad",
    )

    m_own = scatter_blocks([after(m, r_own) for m in m_blocks])
    m_other = swap(m_own, "tensor")
    output = residual + (m_own.astype(WIDE) + m_other.astype(WIDE))

    def to_owners(values):
        width_of = values.shape[1] // owners
        came = []
        for k in range(owners):
            block = lax.dynamic_slice_in_dim(values, (mine ^ k) * width_of, width_of, 1)
            came.append(block if k == 0 else swap(block, "expert", k))
        return came

    normed_columns = to_owners(after(normed, r_own))
    mixed_rows = gather_blocks(after(mixed, r_own))
    low_columns = to_owners(low)
    grad_rows = gather_blocks(grad_qkv)
    shard_out = fold_sum(pair_dot(mixed_rows, low_columns, "out_grad"))
    shard_proj = pair_dot(normed_columns, grad_rows, "proj_grad")
    shard_proj = jnp.concatenate(
        [fold_sum(shard_proj[:, c : c + 256]) for c in range(0, shard_proj.shape[1], 256)], axis=1
    ).astype(WIDE)
    q_cols, k_cols = w_query.shape[1], key_projection.shape[1]

    gains = jnp.concatenate([attn_gain_part, ffn_gain_part], axis=0)
    gains = [
        lax.dynamic_slice_in_dim(gains, (mine ^ k) * shard, shard, 1) for k in range(owners)
    ]
    gains = fold_sum(scatter_blocks(gains))
    grad_gate_w, grad_up_w, grad_down_w = [
        jnp.stack(parts).astype(WIDE) for parts in sums
    ]
    return (
        output.astype(LOW),
        grad_tokens,
        gains[0],
        shard_proj[:, :q_cols],
        shard_proj[:, q_cols : q_cols + k_cols],
        shard_proj[:, q_cols + k_cols :],
        shard_out.astype(WIDE),
        gains[1],
        grad_gate_w,
        grad_up_w,
        grad_down_w,
    )


def solution(mesh):
    placed = (
        P(("dp", "expert"), None),
        P(("dp", "expert")),
        P(("dp", "expert"), None),
        P(("dp", "expert"), None),
        P(("dp", "expert"), None),
        P(),
        P("expert", "tensor"),
        P("expert", "tensor"),
        P("expert", "tensor"),
        P("tensor", "expert"),
        P(),
        P("expert", None, "tensor"),
        P("expert", None, "tensor"),
        P("expert", "tensor", None),
    )
    return jax.shard_map(
        body,
        mesh=mesh,
        in_specs=placed,
        out_specs=(
            P(("dp", "expert"), None),
            P(("dp", "expert"), None),
            P("expert"),
            P("expert", "tensor"),
            P("expert", "tensor"),
            P("expert", "tensor"),
            P("tensor", "expert"),
            P("expert"),
            P("expert", None, "tensor"),
            P("expert", None, "tensor"),
            P("expert", "tensor", None),
        ),
        check_vma=False,
    )
```
